128 devices in a mesh: chan: 16 (over z, y), grp: 8 (over x, core).
Axes of the slice: x: 4, y: 4, z: 4, core: 2. Of those that a mesh axis runs over, the one named last changes fastest.
Arguments:
- voltages: bfloat16 [512, 2, 139, 1024], P(('chan', 'grp')), may hold values from -6 to 6
- filter_taps: float32 [12, 512], replicated, may hold values from -1.75 to 1.75
- chan_index: int32 [192], replicated, may hold values from 0 to 511
- beam_weights: bfloat16 [192, 4096, 2, 512], P('chan', 'grp'), may hold values from -0.1875 to 0.1875
Outputs:
- beams: bfloat16 [192, 4096, 2, 2, 128], P('chan', 'grp')
The draws below stay inside these ranges and needn't reach their ends.
Inputs may be any that keep to these rules, and one draw needn't show every extreme that they name: `chan_index`: filterbank channel numbers; a channel may be selected more than once.
All inputs are finite; a program needn't handle non-finite values.
Results may differ from the reference program's by a relative error of at most 0.0065.
Values may be sent and summed in bfloat16 or wider, within the bound.
A program may use at most 192 MiB of HBM per device.

```python
import math
import jax
import jax.numpy as jnp
from jax import lax

STATIONS = 512
POLS = 2
NFFT = 512
TAPS = 12
BEAMS = 4096
NSEL = 192
BLOCKS = 139


def place_ends(values, stream_key, least, high):
    longest = values.shape.index(max(values.shape))
    spots = []
    for shift in (0, 1):
        where = [jax.random.randint(jax.random.fold_in(stream_key, axis), (), 0, length) for axis, length in enumerate(values.shape)]
        where[longest] = (where[longest] + shift) % values.shape[longest]
        spots.append(tuple(where))
    return values.at[spots[0]].set(least).at[spots[1]].set(high)


def block_levels(rng, extent, pieces, smallest, largest):
    gain = 1.0
    for dim, blocks in pieces:
        draws = jax.random.uniform(jax.random.fold_in(jax.random.fold_in(rng, 6), dim), (blocks,), jnp.float32, smallest / len(pieces), largest / len(pieces))
        gain = gain * jnp.repeat(jnp.exp(draws), extent[dim] // blocks).reshape((-1,) + (1,) * (len(extent) - 1 - dim))
    return gain


def noise(rng, shape, deviation, limit, shards=(), kind=jnp.bfloat16):
    entries = deviation * jax.random.normal(rng, shape, jnp.float32)
    if shards:
        entries = entries * block_levels(rng, shape, shards, -0.22, 0.18)
    return jnp.clip(entries, -limit, limit).astype(kind)


def setup_inputs(seed: int = 0) -> dict:
    keys = jax.random.split(jax.random.key(seed), 5)
    voltages = noise(keys[0], (STATIONS, POLS, BLOCKS, 2 * NFFT), 1.0, 6.0, ((0, 128),))
    filter_taps = noise(keys[1], (TAPS, NFFT), TAPS ** -0.5, 1.75, (), jnp.float32)
    chan_index = place_ends(jax.random.randint(keys[2], (NSEL,), 0, NFFT), jax.random.fold_in(keys[2], 1), 0, NFFT - 1).astype(jnp.int32)
    beam_weights = noise(keys[3], (NSEL, BEAMS, 2, STATIONS), (2 * STATIONS) ** -0.5, 0.1875, ((0, 16), (1, 8)))
    return dict(voltages=voltages, filter_taps=filter_taps, chan_index=chan_index, beam_weights=beam_weights)


def build_table(chan_index, fft_size):
    position = jnp.arange(fft_size, dtype=jnp.int32)
    phase = position[:, None] * chan_index[None, :].astype(jnp.int32) % fft_size
    angle = 2.0 * math.pi / fft_size * phase.astype(jnp.float32)
    factor = 1.0 / math.sqrt(fft_size)
    cosine = jnp.cos(angle) * factor
    sine = jnp.sin(angle) * factor
    upper = jnp.concatenate([cosine, -sine], axis=1)
    lower = jnp.concatenate([sine, cosine], axis=1)
    return jnp.concatenate([upper, lower], axis=0).astype(jnp.bfloat16)

def channelize(voltages, filter_taps, phase_table):
    tap_count = filter_taps.shape[0]
    spectra_count = voltages.shape[2] - tap_count + 1
    doubled = jnp.concatenate([filter_taps, filter_taps], axis=1)
    filtered = jnp.zeros(voltages.shape[:2] + (spectra_count, voltages.shape[3]), jnp.float32)
    for tap_delay in range(tap_count):
        window = voltages[:, :, tap_delay:tap_delay + spectra_count, :].astype(jnp.float32)
        filtered = filtered + window * doubled[tap_delay]
    filtered = filtered.astype(jnp.bfloat16)
    flat = filtered.reshape(-1, filtered.shape[3])
    result = jnp.dot(flat, phase_table, preferred_element_type=jnp.float32).astype(jnp.bfloat16)
    return result.reshape(voltages.shape[:2] + (spectra_count, 2, phase_table.shape[1] // 2))

def reference(voltages, filter_taps, chan_index, beam_weights):
    phase_table = build_table(chan_index, NFFT)
    grouped = voltages.reshape((STATIONS // 16, 16) + voltages.shape[1:])
    spectra = lax.map(lambda station_block: channelize(station_block, filter_taps, phase_table), grouped)
    spectra = spectra.reshape((STATIONS,) + spectra.shape[2:])
    by_channel = jnp.moveaxis(spectra, 4, 0)

    def one_channel(pair):
        weight_block, channel_data = pair
        summed = jnp.einsum('bws,spmr->bwprm', weight_block.astype(jnp.float32), channel_data.astype(jnp.float32), precision=lax.Precision.HIGHEST)
        real_part = summed[:, 0, :, 0] - summed[:, 1, :, 1]
        imag_part = summed[:, 0, :, 1] + summed[:, 1, :, 0]
        return jnp.stack([real_part, imag_part], axis=2).astype(jnp.bfloat16)
    return lax.map(one_channel, (beam_weights, by_channel))
```

```python
import functools
import math

import jax
import jax.numpy as jnp
import numpy as np
from jax import lax
from jax.experimental import pallas as pl
from jax.experimental.pallas import tpu as pltpu
from jax.sharding import PartitionSpec as P

MESH = pl.DeviceIdType.MESH
LANES = 128
CHUNKS = 4


def fourier_rows(size):
    steps = np.arange(size, dtype=np.int64)
    phase = (steps[:, None] * steps[None, :]) % size
    angle = np.float32(2.0 * math.pi / size) * phase.astype(np.float32)
    factor = np.float32(1.0 / math.sqrt(size))
    rows = np.concatenate([np.cos(angle) * factor, np.sin(angle) * factor], axis=1)
    return rows.astype(jnp.bfloat16)


def spectra_kernel(
    dims, volts_hbm, taps_ref, index_ref, rows_ref, out_ref,
    volts, tapb, table, sums, flat, spread, ready,
    load_sem, own_sem, one_send, one_recv, side_send, side_recv, far_send, far_recv, mate_send, mate_recv,
):
    n_chan, n_x, stations, pols, blocks, taps, size, channels = dims
    n_grp = 2 * n_x
    spectra = blocks - taps + 1
    tiles = size // LANES
    per = channels // n_chan
    step = per // CHUNKS
    quads = 2 * pols
    rows_m = 2 * tiles * pols

    chan = lax.axis_index("chan")
    grp = lax.axis_index("grp")
    place = grp // 2
    core = grp % 2
    right = lax.rem(place + 1, n_x) * 2 + core
    left = lax.rem(place + n_x - 1, n_x) * 2 + core
    across = lax.rem(place + 2, n_x) * 2 + core
    mate = place * 2 + 1 - core

    def load(s):
        span = pl.ds(s * blocks * rows_m, blocks * rows_m)
        return pltpu.make_async_copy(volts_hbm.at[span], volts.at[span], load_sem.at[s])

    for s in range(stations):
        load(s).start()

    barrier = pltpu.get_barrier_semaphore()

    def greet(j, carry):
        other = lax.rem(chan + j, n_chan)
        pl.semaphore_signal(barrier, inc=1, device_id={"chan": other, "grp": grp}, device_id_type=MESH)
        return carry

    lax.fori_loop(1, n_chan, greet, 0)
    for other in (right, left, mate):
        pl.semaphore_signal(barrier, inc=1, device_id={"chan": chan, "grp": other}, device_id_type=MESH)

    for t in range(taps):
        for tile in range(tiles):
            line = taps_ref[pl.ds(t, 1), pl.ds(tile * LANES, LANES)]
            tapb[pl.ds((t * tiles + tile) * pols, pols), :] = jnp.broadcast_to(line, (pols, LANES))

    place_of = lax.broadcasted_iota(jnp.int32, (channels, size), 1)
    chosen = (place_of == index_ref[...]).astype(jnp.float32).astype(jnp.bfloat16)
    picked = jnp.dot(chosen, rows_ref[...], preferred_element_type=jnp.float32)
    table[pl.ds(0, channels), :] = picked.astype(jnp.bfloat16)
    table[pl.ds(channels, channels), pl.ds(0, size)] = (-picked[:, size:]).astype(jnp.bfloat16)
    table[pl.ds(channels, channels), pl.ds(size, size)] = picked[:, :size].astype(jnp.bfloat16)

    group = 8
    half = tiles * pols
    for s in range(stations):
        load(s).wait()

        def filter_group(i, carry):
            first = i * group
            coefs = [tapb[pl.ds(t * half, half), :] for t in range(taps)]
            views = []
            for m in range(group + taps - 1):
                start = pl.multiple_of((s * blocks + first + m) * rows_m, rows_m)
                views.append(volts[pl.ds(start, rows_m), :].astype(jnp.float32))
            for m in range(group):
                for part in range(2):
                    total = None
                    for t in range(taps):
                        term = views[m + t][part * half : (part + 1) * half] * coefs[t]
                        total = term if total is None else total + term
                    at = pl.multiple_of((first + m) * rows_m, rows_m) + part * half
                    sums[pl.ds(at, half), :] = total
            return carry

        lax.fori_loop(0, spectra // group, filter_group, 0)
        for p in range(pols):
            for part in range(2):
                for tile in range(tiles):
                    line = part * half + tile * pols + p
                    flat[pl.ds(p * spectra, spectra), pl.ds((part * tiles + tile) * LANES, LANES)] = sums[
                        pl.ds(line, spectra, stride=rows_m), :
                    ].astype(jnp.bfloat16)
        product = lax.dot_general(
            table[...], flat[...], (((1,), (1,)), ((), ())), preferred_element_type=jnp.float32
        )
        for p in range(pols):
            for part in range(2):
                spread[pl.ds((p * 2 + part) * stations + s, channels, stride=quads * stations), :] = product[
                    part * channels : (part + 1) * channels, p * spectra : (p + 1) * spectra
                ]

    packed = ready.reshape(channels * quads * stations, LANES)

    def pack(k, carry):
        wide = spread[pl.ds(pl.multiple_of(k * 64, 64), 64), :].astype(jnp.bfloat16)
        packed[pl.ds(pl.multiple_of(k * 64, 64), 64), :] = wide
        return carry

    lax.fori_loop(0, channels * quads * stations // 64, pack, 0)

    outgoing = ready.reshape(n_chan, per, quads, stations, LANES)
    pl.semaphore_wait(barrier, n_chan + 2)

    def span(i):
        return pl.ds(i * step, step)

    def first_copy(i, other):
        return pltpu.make_async_remote_copy(
            src_ref=outgoing.at[other, span(i)],
            dst_ref=out_ref.at[span(i), :, chan, grp],
            send_sem=one_send.at[i],
            recv_sem=one_recv.at[i],
            device_id={"chan": other, "grp": grp},
            device_id_type=MESH,
        )

    def own_copy(i):
        return pltpu.make_async_copy(outgoing.at[chan, span(i)], out_ref.at[span(i), :, chan, grp], own_sem.at[i])

    for i in range(CHUNKS):
        own_copy(i).start()

        def send(j, carry):
            first_copy(i, lax.rem(chan + j, n_chan)).start()
            return carry

        lax.fori_loop(1, n_chan, send, 0)

    def grp_copy(i, part, owner, to, send_sem, recv_sem):
        if part is None:
            piece = out_ref.at[span(i), :, :, owner]
        else:
            piece = out_ref.at[span(i), pl.ds(part * pols, pols), :, owner]
        return pltpu.make_async_remote_copy(
            src_ref=piece, dst_ref=piece, send_sem=send_sem, recv_sem=recv_sem,
            device_id={"chan": chan, "grp": to}, device_id_type=MESH,
        )

    def side(i, d):
        return grp_copy(i, None, grp, (right, left)[d], side_send.at[i, d], side_recv.at[i, d])

    def side_in(i, d):
        return grp_copy(i, None, (left, right)[d], right, side_send.at[i, d], side_recv.at[i, d])

    def far(i, d):
        return grp_copy(i, d, (left, right)[d], (right, left)[d], far_send.at[i, d], far_recv.at[i, d])

    def far_in(i, d):
        return grp_copy(i, d, across, right, far_send.at[i, d], far_recv.at[i, d])

    def mate_copy(i, e):
        if e == 0:
            return grp_copy(i, None, grp, mate, mate_send.at[i, e], mate_recv.at[i, e])
        if e < 3:
            return grp_copy(i, None, (left, right)[e - 1], mate, mate_send.at[i, e], mate_recv.at[i, e])
        return grp_copy(i, e - 3, across, mate, mate_send.at[i, e], mate_recv.at[i, e])

    def mate_in(i, e):
        shift = 1 - 2 * core
        if e == 0:
            return grp_copy(i, None, mate, mate, mate_send.at[i, e], mate_recv.at[i, e])
        if e < 3:
            return grp_copy(i, None, (left, right)[e - 1] + shift, mate, mate_send.at[i, e], mate_recv.at[i, e])
        return grp_copy(i, e - 3, across + shift, mate, mate_send.at[i, e], mate_recv.at[i, e])

    def gathered(i):
        piece = out_ref.at[span(i), :, pl.ds(0, n_chan - 1), grp]
        return pltpu.make_async_copy(piece, piece, one_recv.at[i])

    def sent(i):
        piece = outgoing.at[pl.ds(0, n_chan - 1), span(i)]
        return pltpu.make_async_copy(piece, piece, one_send.at[i])

    for t in range(CHUNKS + 2):
        if t < CHUNKS:
            own_copy(t).wait()
            gathered(t).wait()
            for d in range(2):
                side(t, d).start()
            mate_copy(t, 0).start()
        i = t - 1
        if 0 <= i < CHUNKS:
            for d in range(2):
                side_in(i, d).wait_recv()
                far(i, d).start()
                mate_copy(i, 1 + d).start()
        i = t - 2
        if 0 <= i < CHUNKS:
            for d in range(2):
                far_in(i, d).wait_recv()
                mate_copy(i, 3 + d).start()
    for i in range(CHUNKS):
        sent(i).wait()
        for d in range(2):
            side(i, d).wait_send()
            far(i, d).wait_send()
        for e in range(5):
            mate_copy(i, e).wait_send()
            mate_in(i, e).wait_recv()


def beams_kernel(dims, weights_ref, spectra_ref, out_ref, wide, ordered, values):
    beams, stations, pols, spectra = dims
    tiles = stations // LANES
    rows_b = 2 * tiles
    group = 64
    for i in range(beams // group):
        wide[pl.ds(i * group * rows_b, group * rows_b), :] = weights_ref[
            pl.ds(i * group * rows_b, group * rows_b), :
        ].astype(jnp.float32)
    for w in range(2):
        for tile in range(tiles):
            ordered[:, pl.ds((w * tiles + tile) * LANES, LANES)] = wide[
                pl.ds(tile * 2 + w, beams, stride=rows_b), :
            ].astype(jnp.bfloat16)
    real = jnp.concatenate([spectra_ref[0, p * 2] for p in range(pols)], axis=1)
    imag = jnp.concatenate([spectra_ref[0, p * 2 + 1] for p in range(pols)], axis=1)
    weights = ordered[...]
    for part in range(2):
        other = jnp.concatenate([imag, real] if part else [real, -imag], axis=0)
        product = jnp.dot(weights, other, preferred_element_type=jnp.float32)
        for p in range(pols):
            values[pl.ds(p * 2 + part, beams, stride=2 * pols), :] = product[:, p * spectra : (p + 1) * spectra]
    out_ref[...] = values[...].astype(jnp.bfloat16)


def shards(sizes, voltages, filter_taps, chan_index, beam_weights):
    n_chan, n_grp = sizes
    stations, pols, blocks, width = voltages.shape
    taps, size = filter_taps.shape
    channels = chan_index.shape[0]
    per, beams = beam_weights.shape[:2]
    everyone = beam_weights.shape[3]
    spectra = blocks - taps + 1
    tiles = size // LANES
    rows_m = 2 * tiles * pols
    quads = 2 * pols

    lines = voltages.transpose(0, 2, 1, 3).reshape(stations, blocks, pols, 2 * tiles, LANES)
    lines = lines.transpose(0, 1, 3, 2, 4).reshape(stations * blocks * rows_m, LANES)
    index = chan_index.reshape(channels, 1)
    dims = (n_chan, n_grp // 2, stations, pols, blocks, taps, size, channels)
    spread_rows = channels * quads * stations
    dma = pltpu.SemaphoreType.DMA
    held = pl.pallas_call(
        functools.partial(spectra_kernel, dims),
        out_shape=jax.ShapeDtypeStruct((per, quads, n_chan, n_grp, stations, LANES), jnp.bfloat16),
        in_specs=[
            pl.BlockSpec(memory_space=pl.ANY),
            pl.BlockSpec(memory_space=pltpu.VMEM),
            pl.BlockSpec(memory_space=pltpu.VMEM),
            pl.BlockSpec(memory_space=pltpu.VMEM),
        ],
        out_specs=pl.BlockSpec(memory_space=pl.ANY),
        scratch_shapes=[
            pltpu.VMEM((stations * blocks * rows_m, LANES), jnp.bfloat16),
            pltpu.VMEM((taps * tiles * pols, LANES), jnp.float32),
            pltpu.VMEM((2 * channels, 2 * size), jnp.bfloat16),
            pltpu.VMEM((spectra * rows_m, LANES), jnp.float32),
            pltpu.VMEM((pols * spectra, 2 * size), jnp.bfloat16),
            pltpu.VMEM((spread_rows, LANES), jnp.float32),
            pltpu.VMEM((spread_rows // stations, stations, LANES), jnp.bfloat16),
            dma((stations,)), dma((CHUNKS,)), dma((CHUNKS,)), dma((CHUNKS,)),
            dma((CHUNKS, 2)), dma((CHUNKS, 2)), dma((CHUNKS, 2)), dma((CHUNKS, 2)),
            dma((CHUNKS, 5)), dma((CHUNKS, 5)),
        ],
        compiler_params=pltpu.CompilerParams(
            collective_id=0, has_side_effects=True, vmem_limit_bytes=48 * 1024 * 1024
        ),
        name="spectra",
    )(lines, filter_taps, index, jnp.asarray(fourier_rows(size)))

    held = held.reshape(per, quads, everyone, LANES)
    tiles_s = everyone // LANES
    rows_w = beam_weights.reshape(per, beams, 2, tiles_s, LANES).transpose(0, 1, 3, 2, 4)
    rows_w = rows_w.reshape(per * beams * tiles_s * 2, LANES)
    beam_rows = beams * tiles_s * 2
    out = pl.pallas_call(
        functools.partial(beams_kernel, (beams, everyone, pols, spectra)),
        out_shape=jax.ShapeDtypeStruct((per * beams * quads, LANES), jnp.bfloat16),
        grid=(per,),
        in_specs=[
            pl.BlockSpec((beam_rows, LANES), lambda k: (k, 0)),
            pl.BlockSpec((1, quads, everyone, LANES), lambda k: (k, 0, 0, 0)),
        ],
        out_specs=pl.BlockSpec((beams * quads, LANES), lambda k: (k, 0)),
        scratch_shapes=[
            pltpu.VMEM((beam_rows, LANES), jnp.float32),
            pltpu.VMEM((beams, 2 * everyone), jnp.bfloat16),
            pltpu.VMEM((beams * quads, LANES), jnp.float32),
        ],
        compiler_params=pltpu.CompilerParams(vmem_limit_bytes=48 * 1024 * 1024),
        name="beams",
    )(rows_w, held)
    return out.reshape(per, beams, pols, 2, spectra)


def solution(mesh):
    sizes = (mesh.shape["chan"], mesh.shape["grp"])
    placed = (P(("chan", "grp"), None, None, None), P(), P(), P("chan", "grp", None, None))
    return jax.shard_map(
        functools.partial(shards, sizes),
        mesh=mesh,
        in_specs=placed,
        out_specs=P("chan", "grp", None, None, None),
        check_vma=False,
    )
```

```python
import functools
import math

import jax
import jax.numpy as jnp
import numpy as np
from jax import lax
from jax.experimental import pallas as pl
from jax.experimental.pallas import tpu as pltpu
from jax.sharding import PartitionSpec as P

MESH = pl.DeviceIdType.MESH
LANES = 128
CHUNKS = 6
LATE = 4


def fourier_rows(size):
    steps = np.arange(size, dtype=np.int64)
    phase = (steps[:, None] * steps[None, :]) % size
    angle = np.float32(2.0 * math.pi / size) * phase.astype(np.float32)
    factor = np.float32(1.0 / math.sqrt(size))
    rows = np.concatenate([np.cos(angle) * factor, np.sin(angle) * factor], axis=1)
    return rows.astype(jnp.bfloat16)


def spectra_kernel(
    dims, volts_hbm, taps_hbm, index_ref, rows_hbm, weights_hbm, part_ref, late_ref, late_weights_ref,
    volts, taps_ref, rows_ref, tapb, table, sums, flat, spread, ready, held, raw, wide, ordered, values, done,
    load_sem, own_sem, one_send, one_recv, side_send, side_recv, far_send, far_recv, mate_send, mate_recv,
    raw_sem, part_sem, late_sem, late_weights_sem,
):
    n_chan, n_x, stations, pols, blocks, taps, size, channels, beams, late = dims
    n_grp = 2 * n_x
    spectra = blocks - taps + 1
    tiles = size // LANES
    per = channels // n_chan
    step = per // CHUNKS
    early = per - late
    quads = 2 * pols
    rows_m = 2 * tiles * pols
    everyone = n_chan * n_grp * stations
    tiles_s = everyone // LANES
    rows_b = 2 * tiles_s
    rows_w = beams * rows_b
    rows_o = beams * quads

    chan = lax.axis_index("chan")
    grp = lax.axis_index("grp")
    place = grp // 2
    core = grp % 2
    right = lax.rem(place + 1, n_x) * 2 + core
    left = lax.rem(place + n_x - 1, n_x) * 2 + core
    across = lax.rem(place + 2, n_x) * 2 + core
    mate = place * 2 + 1 - core

    def load(s):
        span = pl.ds(s * blocks * rows_m, blocks * rows_m)
        return pltpu.make_async_copy(volts_hbm.at[span], volts.at[span], load_sem.at[s])

    def load_taps():
        return pltpu.make_async_copy(taps_hbm, taps_ref, load_sem.at[stations])

    def load_rows():
        return pltpu.make_async_copy(rows_hbm, rows_ref, load_sem.at[stations + 1])

    load_taps().start()
    load(0).start()
    load_rows().start()
    for s in range(1, stations):
        load(s).start()

    barrier = pltpu.get_barrier_semaphore()

    def greet(j, carry):
        other = lax.rem(chan + j, n_chan)
        pl.semaphore_signal(barrier, inc=1, device_id={"chan": other, "grp": grp}, device_id_type=MESH)
        return carry

    lax.fori_loop(1, n_chan, greet, 0)
    for other in (right, left, mate):
        pl.semaphore_signal(barrier, inc=1, device_id={"chan": chan, "grp": other}, device_id_type=MESH)

    load_taps().wait()
    for t in range(taps):
        for tile in range(tiles):
            line = taps_ref[pl.ds(t, 1), pl.ds(tile * LANES, LANES)]
            tapb[pl.ds((t * tiles + tile) * pols, pols), :] = jnp.broadcast_to(line, (pols, LANES))

    load_rows().wait()
    place_of = lax.broadcasted_iota(jnp.int32, (size, channels), 0)
    chosen = (place_of == index_ref[...]).astype(jnp.float32).astype(jnp.bfloat16)
    picked = lax.dot_general(
        chosen, rows_ref[...], (((0,), (0,)), ((), ())), preferred_element_type=jnp.float32
    )
    table[pl.ds(0, channels), :] = picked.astype(jnp.bfloat16)
    table[pl.ds(channels, channels), pl.ds(0, size)] = (-picked[:, size:]).astype(jnp.bfloat16)
    table[pl.ds(channels, channels), pl.ds(size, size)] = picked[:, :size].astype(jnp.bfloat16)

    group = 8
    half = tiles * pols
    for s in range(stations):
        load(s).wait()

        def filter_group(i, carry):
            first = i * group
            coefs = [tapb[pl.ds(t * half, half), :] for t in range(taps)]
            views = []
            for m in range(group + taps - 1):
                start = pl.multiple_of((s * blocks + first + m) * rows_m, rows_m)
                views.append(volts[pl.ds(start, rows_m), :].astype(jnp.float32))
            for m in range(group):
                for part in range(2):
                    total = None
                    for t in range(taps):
                        term = views[m + t][part * half : (part + 1) * half] * coefs[t]
                        total = term if total is None else total + term
                    at = pl.multiple_of((first + m) * rows_m, rows_m) + part * half
                    sums[pl.ds(at, half), :] = total
            return carry

        lax.fori_loop(0, spectra // group, filter_group, 0)
        for p in range(pols):
            for part in range(2):
                for tile in range(tiles):
                    line = part * half + tile * pols + p
                    flat[pl.ds(p * spectra, spectra), pl.ds((part * tiles + tile) * LANES, LANES)] = sums[
                        pl.ds(line, spectra, stride=rows_m), :
                    ].astype(jnp.bfloat16)
        product = sum(
            lax.dot_general(
                table[:, part * size : (part + 1) * size],
                flat[:, part * size : (part + 1) * size],
                (((1,), (1,)), ((), ())),
                preferred_element_type=jnp.float32,
            )
            for part in range(2)
        )
        for p in range(pols):
            for part in range(2):
                spread[pl.ds((p * 2 + part) * stations + s, channels, stride=quads * stations), :] = product[
                    part * channels : (part + 1) * channels, p * spectra : (p + 1) * spectra
                ]

    packed = ready.reshape(channels * quads * stations, LANES)

    def pack(k, carry):
        wider = spread[pl.ds(pl.multiple_of(k * 64, 64), 64), :].astype(jnp.bfloat16)
        packed[pl.ds(pl.multiple_of(k * 64, 64), 64), :] = wider
        return carry

    lax.fori_loop(0, channels * quads * stations // 64, pack, 0)

    outgoing = ready.reshape(n_chan, per, quads, stations, LANES)
    pl.semaphore_wait(barrier, n_chan + 2)

    def span(i):
        return pl.ds(i * step, step)

    def first_copy(i, other):
        return pltpu.make_async_remote_copy(
            src_ref=outgoing.at[other, span(i)],
            dst_ref=held.at[span(i), :, chan, grp],
            send_sem=one_send.at[i],
            recv_sem=one_recv.at[i],
            device_id={"chan": other, "grp": grp},
            device_id_type=MESH,
        )

    def own_copy(i):
        return pltpu.make_async_copy(outgoing.at[chan, span(i)], held.at[span(i), :, chan, grp], own_sem.at[i])

    def first_sends(i, carry):
        own_copy(i).start()

        def send(j, carry):
            first_copy(i, lax.rem(chan + j, n_chan)).start()
            return carry

        return lax.fori_loop(1, n_chan, send, carry)

    lax.fori_loop(0, CHUNKS, first_sends, 0)

    def grp_copy(i, part, owner, to, send_sem, recv_sem):
        if part is None:
            piece = held.at[span(i), :, :, owner]
        else:
            piece = held.at[span(i), pl.ds(part * pols, pols), :, owner]
        return pltpu.make_async_remote_copy(
            src_ref=piece, dst_ref=piece, send_sem=send_sem, recv_sem=recv_sem,
            device_id={"chan": chan, "grp": to}, device_id_type=MESH,
        )

    def side(i, d):
        return grp_copy(i, None, grp, (right, left)[d], side_send.at[i, d], side_recv.at[i, d])

    def side_in(i, d):
        return grp_copy(i, None, (left, right)[d], right, side_send.at[i, d], side_recv.at[i, d])

    def far(i, d):
        return grp_copy(i, d, (left, right)[d], (right, left)[d], far_send.at[i, d], far_recv.at[i, d])

    def far_in(i, d):
        return grp_copy(i, d, across, right, far_send.at[i, d], far_recv.at[i, d])

    def mate_copy(i, e):
        sems = (mate_send.at[i, e], mate_recv.at[i, e])
        if e == 0:
            return grp_copy(i, None, grp, mate, *sems)
        if e < 3:
            return grp_copy(i, None, (left, right)[e - 1], mate, *sems)
        return grp_copy(i, e - 3, across, mate, *sems)

    def mate_in(i, e):
        shift = 1 - 2 * core
        sems = (mate_send.at[i, e], mate_recv.at[i, e])
        if e == 0:
            return grp_copy(i, None, mate, mate, *sems)
        if e < 3:
            return grp_copy(i, None, (left, right)[e - 1] + shift, mate, *sems)
        return grp_copy(i, e - 3, across + shift, mate, *sems)

    def gathered(i):
        piece = held.at[span(i), :, pl.ds(0, n_chan - 1), grp]
        return pltpu.make_async_copy(piece, piece, one_recv.at[i])

    def sent(i):
        piece = outgoing.at[pl.ds(0, n_chan - 1), span(i)]
        return pltpu.make_async_copy(piece, piece, one_send.at[i])

    def load_raw(k):
        return pltpu.make_async_copy(
            weights_hbm.at[pl.ds(pl.multiple_of(k * rows_w, rows_w), rows_w)], raw.at[k % 2], raw_sem.at[k % 2]
        )

    def late_weights(k):
        return pltpu.make_async_copy(ordered.at[k], late_weights_ref.at[k - early], late_weights_sem.at[k - early])

    def late_spectra(i):
        where = pl.ds(i * step - early, step)
        return pltpu.make_async_copy(held.at[span(i)], late_ref.at[where], late_sem.at[i])

    def order(k, carry):
        load_raw(k).wait()

        @pl.when(k + 1 < per)
        def _():
            load_raw(k + 1).start()

        wide[...] = raw[k % 2].astype(jnp.float32)
        for w in range(2):
            for tile in range(tiles_s):
                ordered[k, :, pl.ds((w * tiles_s + tile) * LANES, LANES)] = wide[
                    pl.ds(tile * 2 + w, beams, stride=rows_b), :
                ].astype(jnp.bfloat16)

        @pl.when(k >= early)
        def _():
            late_weights(k).start()

        return carry

    lines = held.reshape(per * quads * everyone, LANES)

    def put(k):
        return pltpu.make_async_copy(
            done.at[k % 2], part_ref.at[pl.ds(pl.multiple_of(k * rows_o, rows_o), rows_o)], part_sem.at[k % 2]
        )

    def form(k, carry):
        quad = [
            lines[pl.ds(pl.multiple_of((k * quads + q) * everyone, everyone), everyone), :] for q in range(quads)
        ]
        form_beams(quad, ordered[k], values, beams, pols, spectra)

        @pl.when(k >= 2)
        def _():
            put(k).wait()

        done[k % 2] = values[...].astype(jnp.bfloat16)
        put(k).start()
        return carry

    load_raw(0).start()

    def turn(t, carry):
        @pl.when(t < CHUNKS)
        def _():
            lax.fori_loop(t * step, (t + 1) * step, order, 0)
            own_copy(t).wait()
            gathered(t).wait()
            for d in range(2):
                side(t, d).start()
            mate_copy(t, 0).start()

        @pl.when((t >= 1) & (t < CHUNKS + 1))
        def _():
            for d in range(2):
                side_in(t - 1, d).wait_recv()
                far(t - 1, d).start()
                mate_copy(t - 1, 1 + d).start()

        @pl.when((t >= 2) & (t < CHUNKS + 2))
        def _():
            for d in range(2):
                far_in(t - 2, d).wait_recv()
                mate_copy(t - 2, 3 + d).start()

        @pl.when((t >= 3) & (t < CHUNKS + 3))
        def _():
            for e in range(5):
                mate_in(t - 3, e).wait_recv()

            @pl.when(t - 3 >= early // step)
            def _():
                late_spectra(t - 3).start()

            @pl.when(t - 3 < early // step)
            def _():
                lax.fori_loop((t - 3) * step, (t - 2) * step, form, 0)

        return carry

    lax.fori_loop(0, CHUNKS + 3, turn, 0)

    def finish(i, carry):
        sent(i).wait()
        for d in range(2):
            side(i, d).wait_send()
            far(i, d).wait_send()
        for e in range(5):
            mate_copy(i, e).wait_send()
        return carry

    lax.fori_loop(0, CHUNKS, finish, 0)
    for k in range(early - 2, early):
        put(k).wait()
    for k in range(early, per):
        late_weights(k).wait()
    for i in range(early // step, CHUNKS):
        late_spectra(i).wait()


def form_beams(quad, weights, values, beams, pols, spectra):
    real = jnp.concatenate([quad[p * 2] for p in range(pols)], axis=1)
    imag = jnp.concatenate([quad[p * 2 + 1] for p in range(pols)], axis=1)
    for part in range(2):
        other = jnp.concatenate([imag, real] if part else [real, -imag], axis=0)
        product = jnp.dot(weights, other, preferred_element_type=jnp.float32)
        for p in range(pols):
            values[pl.ds(p * 2 + part, beams, stride=2 * pols), :] = product[:, p * spectra : (p + 1) * spectra]


def beams_kernel(
    dims, part_hbm, spectra_hbm, weights_hbm, out_ref, part, held, ordered, values, done,
    part_in, part_out, held_sem, ordered_sem, done_sem,
):
    beams, pols, spectra, early, late = dims
    quads = 2 * pols
    rows_o = beams * quads

    def take(k):
        where = pl.ds(k * rows_o, rows_o)
        return pltpu.make_async_copy(part_hbm.at[where], part.at[where], part_in.at[k])

    def give(k):
        where = pl.ds(k * rows_o, rows_o)
        return pltpu.make_async_copy(part.at[where], out_ref.at[where], part_out.at[k])

    def spectra_of(k):
        return pltpu.make_async_copy(spectra_hbm.at[k], held.at[k], held_sem.at[k])

    def weights_of(k):
        return pltpu.make_async_copy(weights_hbm.at[k], ordered.at[k], ordered_sem.at[k])

    def put(k):
        return pltpu.make_async_copy(
            done.at[k], out_ref.at[pl.ds((early + k) * rows_o, rows_o)], done_sem.at[k]
        )

    each = -(-early // late)
    for k in range(late):
        spectra_of(k).start()
        weights_of(k).start()
    for k in range(early):
        take(k).start()
    for k in range(late):
        spectra_of(k).wait()
        weights_of(k).wait()
        form_beams([held[k, q] for q in range(quads)], ordered[k], values, beams, pols, spectra)
        done[k] = values[...].astype(jnp.bfloat16)
        put(k).start()
        for j in range(k * each, min(early, (k + 1) * each)):
            take(j).wait()
            give(j).start()
    for k in range(early):
        give(k).wait()
    for k in range(late):
        put(k).wait()


def shards(sizes, voltages, filter_taps, chan_index, beam_weights):
    n_chan, n_grp = sizes
    stations, pols, blocks, width = voltages.shape
    taps, size = filter_taps.shape
    channels = chan_index.shape[0]
    per, beams = beam_weights.shape[:2]
    everyone = beam_weights.shape[3]
    spectra = blocks - taps + 1
    tiles = size // LANES
    tiles_s = everyone // LANES
    rows_m = 2 * tiles * pols
    quads = 2 * pols
    late = LATE
    early = per - late
    beam_rows = beams * tiles_s * 2
    rows_o = beams * quads

    lines = voltages.transpose(0, 2, 1, 3).reshape(stations, blocks, pols, 2 * tiles, LANES)
    lines = lines.transpose(0, 1, 3, 2, 4).reshape(stations * blocks * rows_m, LANES)
    rows_w = beam_weights.reshape(per, beams, 2, tiles_s, LANES).transpose(0, 1, 3, 2, 4)
    rows_w = rows_w.reshape(per * beam_rows, LANES)
    index = chan_index.reshape(1, channels)
    dims = (n_chan, n_grp // 2, stations, pols, blocks, taps, size, channels, beams, late)
    spread_rows = channels * quads * stations
    dma = pltpu.SemaphoreType.DMA
    anywhere = pl.BlockSpec(memory_space=pl.ANY)
    part, held, ordered = pl.pallas_call(
        functools.partial(spectra_kernel, dims),
        out_shape=[
            jax.ShapeDtypeStruct((early * rows_o, LANES), jnp.bfloat16),
            jax.ShapeDtypeStruct((late, quads, n_chan, n_grp, stations, LANES), jnp.bfloat16),
            jax.ShapeDtypeStruct((late, beams, 2 * everyone), jnp.bfloat16),
        ],
        in_specs=[anywhere, anywhere, pl.BlockSpec(memory_space=pltpu.VMEM), anywhere, anywhere],
        out_specs=[anywhere] * 3,
        scratch_shapes=[
            pltpu.VMEM((stations * blocks * rows_m, LANES), jnp.bfloat16),
            pltpu.VMEM((taps, size), jnp.float32),
            pltpu.VMEM((size, 2 * size), jnp.bfloat16),
            pltpu.VMEM((taps * tiles * pols, LANES), jnp.float32),
            pltpu.VMEM((2 * channels, 2 * size), jnp.bfloat16),
            pltpu.VMEM((spectra * rows_m, LANES), jnp.float32),
            pltpu.VMEM((pols * spectra, 2 * size), jnp.bfloat16),
            pltpu.VMEM((spread_rows, LANES), jnp.float32),
            pltpu.VMEM((spread_rows // stations, stations, LANES), jnp.bfloat16),
            pltpu.VMEM((per, quads, n_chan, n_grp, stations, LANES), jnp.bfloat16),
            pltpu.VMEM((2, beam_rows, LANES), jnp.bfloat16),
            pltpu.VMEM((beam_rows, LANES), jnp.float32),
            pltpu.VMEM((per, beams, 2 * everyone), jnp.bfloat16),
            pltpu.VMEM((rows_o, LANES), jnp.float32),
            pltpu.VMEM((2, rows_o, LANES), jnp.bfloat16),
            dma((stations + 2,)), dma((CHUNKS,)), dma((CHUNKS,)), dma((CHUNKS,)),
            dma((CHUNKS, 2)), dma((CHUNKS, 2)), dma((CHUNKS, 2)), dma((CHUNKS, 2)),
            dma((CHUNKS, 5)), dma((CHUNKS, 5)),
            dma((2,)), dma((2,)), dma((CHUNKS,)), dma((late,)),
        ],
        compiler_params=pltpu.CompilerParams(
            collective_id=0, has_side_effects=True, vmem_limit_bytes=63 * 1024 * 1024
        ),
        name="spectra",
    )(lines, filter_taps, index, jnp.asarray(fourier_rows(size)), rows_w)

    out = pl.pallas_call(
        functools.partial(beams_kernel, (beams, pols, spectra, early, late)),
        out_shape=jax.ShapeDtypeStruct((per * rows_o, LANES), jnp.bfloat16),
        in_specs=[anywhere] * 3,
        out_specs=anywhere,
        scratch_shapes=[
            pltpu.VMEM((early * rows_o, LANES), jnp.bfloat16),
            pltpu.VMEM((late, quads, everyone, LANES), jnp.bfloat16),
            pltpu.VMEM((late, beams, 2 * everyone), jnp.bfloat16),
            pltpu.VMEM((rows_o, LANES), jnp.float32),
            pltpu.VMEM((late, rows_o, LANES), jnp.bfloat16),
            dma((early,)), dma((early,)), dma((late,)), dma((late,)), dma((late,)),
        ],
        compiler_params=pltpu.CompilerParams(vmem_limit_bytes=63 * 1024 * 1024),
        name="beams",
    )(part, held.reshape(late, quads, everyone, LANES), ordered)
    return out.reshape(per, beams, pols, 2, spectra)


def solution(mesh):
    sizes = (mesh.shape["chan"], mesh.shape["grp"])
    placed = (P(("chan", "grp"), None, None, None), P(), P(), P("chan", "grp", None, None))
    return jax.shard_map(
        functools.partial(shards, sizes),
        mesh=mesh,
        in_specs=placed,
        out_specs=P("chan", "grp", None, None, None),
        check_vma=False,
    )
```

```python
import functools
import math

import jax
import jax.numpy as jnp
import numpy as np
from jax import lax
from jax.experimental import pallas as pl
from jax.experimental.pallas import tpu as pltpu
from jax.sharding import PartitionSpec as P

MESH = pl.DeviceIdType.MESH
LANES = 128
ITEMS = ((0, 2), (2, 4), (4, 6), (6, 8), (8, 10), (10, 12))
AHEAD = (0, 1)
TURNS = (
    (("out", 0), ("first", 2), ("out", 1), ("first", 3)),
    (("far", 0), ("out", 2), ("first", 4)),
    (("far", 1), ("out", 3), ("first", 5), ("mate", 0)),
    (("far", 2), ("out", 4), ("mate", 1), ("all", 0)),
    (("far", 3), ("out", 5), ("mate", 2), ("all", 1)),
    (("far", 4), ("mate", 3), ("all", 2)),
    (("far", 5), ("mate", 4), ("all", 3)),
    (("mate", 5), ("late", 4), ("late", 5)),
)
FORMED = (0, 0, 0, 2, 2, 2, 2, 0)
ORDERED = (2, 4, 4, 2, 0, 0, 0, 0)
LATE = 4


def fourier_rows(size):
    steps = np.arange(size, dtype=np.int64)
    phase = (steps[:, None] * steps[None, :]) % size
    angle = np.float32(2.0 * math.pi / size) * phase.astype(np.float32)
    factor = np.float32(1.0 / math.sqrt(size))
    rows = np.concatenate([np.cos(angle) * factor, np.sin(angle) * factor], axis=1)
    return rows.astype(jnp.bfloat16)


def spectra_kernel(
    dims, volts_hbm, taps_hbm, index_ref, rows_hbm, weights_hbm, part_ref, late_ref, late_weights_ref,
    volts, taps_ref, rows_ref, tapb, table, sums, flat, spread, ready, held, raw, wide, ordered, values, done,
    load_sem, own_sem, one_send, one_recv, side_send, side_recv, far_send, far_recv, mate_send, mate_recv,
    raw_sem, part_sem, late_sem, late_weights_sem,
):
    n_chan, n_x, stations, pols, blocks, taps, size, channels, beams, late = dims
    n_grp = 2 * n_x
    spectra = blocks - taps + 1
    tiles = size // LANES
    per = channels // n_chan
    early = per - late
    quads = 2 * pols
    rows_m = 2 * tiles * pols
    everyone = n_chan * n_grp * stations
    tiles_s = everyone // LANES
    rows_b = 2 * tiles_s
    rows_w = beams * rows_b
    rows_o = beams * quads

    chan = lax.axis_index("chan")
    grp = lax.axis_index("grp")
    place = grp // 2
    core = grp % 2
    right = lax.rem(place + 1, n_x) * 2 + core
    left = lax.rem(place + n_x - 1, n_x) * 2 + core
    across = lax.rem(place + 2, n_x) * 2 + core
    mate = place * 2 + 1 - core

    def load(s):
        span = pl.ds(s * blocks * rows_m, blocks * rows_m)
        return pltpu.make_async_copy(volts_hbm.at[span], volts.at[span], load_sem.at[s])

    def load_taps():
        return pltpu.make_async_copy(taps_hbm, taps_ref, load_sem.at[stations])

    def load_rows():
        return pltpu.make_async_copy(rows_hbm, rows_ref, load_sem.at[stations + 1])

    load_taps().start()
    load(0).start()
    load_rows().start()
    for s in range(1, stations):
        load(s).start()

    def load_raw(k):
        return pltpu.make_async_copy(
            weights_hbm.at[pl.ds(pl.multiple_of(k * rows_w, rows_w), rows_w)], raw.at[k % 2], raw_sem.at[k % 2]
        )

    load_raw(0).start(priority=1)

    barrier = pltpu.get_barrier_semaphore()

    def greet(j, carry):
        other = lax.rem(chan + j, n_chan)
        pl.semaphore_signal(barrier, inc=1, device_id={"chan": other, "grp": grp}, device_id_type=MESH)
        return carry

    lax.fori_loop(1, n_chan, greet, 0)
    for other in (right, left, mate):
        pl.semaphore_signal(barrier, inc=1, device_id={"chan": chan, "grp": other}, device_id_type=MESH)

    load_taps().wait()
    for t in range(taps):
        for tile in range(tiles):
            line = taps_ref[pl.ds(t, 1), pl.ds(tile * LANES, LANES)]
            tapb[pl.ds((t * tiles + tile) * pols, pols), :] = jnp.broadcast_to(line, (pols, LANES))

    load_rows().wait()
    place_of = lax.broadcasted_iota(jnp.int32, (size, channels), 0)
    chosen = (place_of == index_ref[...]).astype(jnp.float32).astype(jnp.bfloat16)
    picked = lax.dot_general(
        chosen, rows_ref[...], (((0,), (0,)), ((), ())), preferred_element_type=jnp.float32
    )
    table[pl.ds(0, channels), :] = picked.astype(jnp.bfloat16)
    table[pl.ds(channels, channels), pl.ds(0, size)] = (-picked[:, size:]).astype(jnp.bfloat16)
    table[pl.ds(channels, channels), pl.ds(size, size)] = picked[:, :size].astype(jnp.bfloat16)

    outgoing = ready.reshape(n_chan, per, quads, stations, LANES)
    packed = ready.reshape(channels * quads * stations, LANES)

    def span(i):
        return pl.ds(ITEMS[i][0], ITEMS[i][1] - ITEMS[i][0])

    def first_copy(i, other):
        return pltpu.make_async_remote_copy(
            src_ref=outgoing.at[other, span(i)],
            dst_ref=held.at[span(i), :, chan, grp],
            send_sem=one_send.at[i],
            recv_sem=one_recv.at[i],
            device_id={"chan": other, "grp": grp},
            device_id_type=MESH,
        )

    def own_copy(i):
        return pltpu.make_async_copy(outgoing.at[chan, span(i)], held.at[span(i), :, chan, grp], own_sem.at[i])

    def first_sends(i):
        def send(j, carry):
            first_copy(i, lax.rem(chan + j, n_chan)).start()
            return carry

        lax.fori_loop(1, n_chan, send, 0)
        own_copy(i).start()

    def gathered(i):
        piece = held.at[span(i), :, pl.ds(0, n_chan - 1), grp]
        return pltpu.make_async_copy(piece, piece, one_recv.at[i])

    def sent(i):
        piece = held.at[span(i), :, pl.ds(0, n_chan - 1), grp]
        return pltpu.make_async_copy(piece, piece, one_send.at[i])

    def grp_copy(i, part, owner, to, send_sem, recv_sem):
        quad = slice(None) if part is None else pl.ds(part * pols, pols)
        piece = held.at[span(i), quad, :, owner]
        return pltpu.make_async_remote_copy(
            src_ref=piece, dst_ref=piece, send_sem=send_sem, recv_sem=recv_sem,
            device_id={"chan": chan, "grp": to}, device_id_type=MESH,
        )

    def side(i, d):
        return grp_copy(i, None, grp, (right, left)[d], side_send.at[i, d], side_recv.at[i, d])

    def side_in(i, d):
        return grp_copy(i, None, (left, right)[d], right, side_send.at[i, d], side_recv.at[i, d])

    def far(i, d):
        return grp_copy(i, d, (left, right)[d], (right, left)[d], far_send.at[i, d], far_recv.at[i, d])

    def far_in(i, d):
        return grp_copy(i, d, across, right, far_send.at[i, d], far_recv.at[i, d])

    def mate_copy(i, e):
        sems = (mate_send.at[i, e], mate_recv.at[i, e])
        if e == 0:
            return grp_copy(i, None, grp, mate, *sems)
        if e < 3:
            return grp_copy(i, None, (left, right)[e - 1], mate, *sems)
        return grp_copy(i, e - 3, across, mate, *sems)

    def mate_in(i, e):
        shift = 1 - 2 * core
        sems = (mate_send.at[i, e], mate_recv.at[i, e])
        if e == 0:
            return grp_copy(i, None, mate, mate, *sems)
        if e < 3:
            return grp_copy(i, None, (left, right)[e - 1] + shift, mate, *sems)
        return grp_copy(i, e - 3, across + shift, mate, *sems)

    def late_spectra(i):
        low, high = ITEMS[i]
        return pltpu.make_async_copy(
            held.at[pl.ds(low, high - low)], late_ref.at[pl.ds(low - early, high - low)], late_sem.at[i]
        )

    def out(i):
        own_copy(i).wait()
        gathered(i).wait()
        for d in range(2):
            side(i, d).start()
        mate_copy(i, 0).start()

    def act(what, i):
        if what == "out":
            out(i)
        if what == "first":
            first_sends(i)
        for d in range(2):
            if what == "far":
                side_in(i, d).wait_recv()
                far(i, d).start()
                mate_copy(i, 1 + d).start()
            if what == "mate":
                far_in(i, d).wait_recv()
                mate_copy(i, 3 + d).start()
        if what in ("all", "late"):
            for e in range(5):
                mate_in(i, e).wait_recv()
        if what == "late":
            late_spectra(i).start(priority=1)

    group = 8
    half = tiles * pols
    for s in range(stations):
        load(s).wait()

        def filter_group(i, carry):
            first = i * group
            coefs = [tapb[pl.ds(t * half, half), :] for t in range(taps)]
            views = []
            for m in range(group + taps - 1):
                start = pl.multiple_of((s * blocks + first + m) * rows_m, rows_m)
                views.append(volts[pl.ds(start, rows_m), :].astype(jnp.float32))
            both = [coefs[2 * j] + coefs[2 * j + 1] for j in range(taps // 2)]
            for part in range(2):
                side_of = [view[part * half : (part + 1) * half] for view in views]

                def chain(values, factors):
                    total = values[0] * factors[0]
                    for value, factor in zip(values[1:], factors[1:]):
                        total = total + value * factor
                    return total

                joined = [side_of[m] + side_of[m + 1] for m in range(1, group + taps - 2, 2)]
                before_it = chain(side_of[0 : taps : 2], coefs[0::2])
                for i in range(group // 2):
                    odd = chain(side_of[2 * i + 1 : 2 * i + 1 + taps : 2], coefs[1::2])
                    after_it = chain(side_of[2 * i + 2 : 2 * i + 2 + taps : 2][: taps // 2], coefs[0::2])
                    cross = chain(joined[i : i + taps // 2], both)
                    for m, total in ((0, before_it + odd), (1, (cross - odd) - after_it)):
                        at = pl.multiple_of((first + 2 * i + m) * rows_m, rows_m) + part * half
                        sums[pl.ds(at, half), :] = total
                    before_it = after_it
            return carry

        lax.fori_loop(0, spectra // group, filter_group, 0)
        for p in range(pols):
            for part in range(2):
                for tile in range(tiles):
                    line = part * half + tile * pols + p
                    flat[pl.ds(p * spectra, spectra), pl.ds((part * tiles + tile) * LANES, LANES)] = sums[
                        pl.ds(line, spectra, stride=rows_m), :
                    ].astype(jnp.bfloat16)
        product = sum(
            lax.dot_general(
                table[:, part * size : (part + 1) * size],
                flat[:, part * size : (part + 1) * size],
                (((1,), (1,)), ((), ())),
                preferred_element_type=jnp.float32,
            )
            for part in range(2)
        )
        for p in range(pols):
            for part in range(2):
                spread[pl.ds((p * 2 + part) * stations + s, channels, stride=quads * stations), :] = product[
                    part * channels : (part + 1) * channels, p * spectra : (p + 1) * spectra
                ]

    def pack(k, carry):
        wider = spread[pl.ds(pl.multiple_of(k * 64, 64), 64), :].astype(jnp.bfloat16)
        packed[pl.ds(pl.multiple_of(k * 64, 64), 64), :] = wider
        return carry

    lax.fori_loop(0, channels * quads * stations // 64, pack, 0)
    pl.semaphore_wait(barrier, n_chan + 2)
    for i in AHEAD:
        first_sends(i)

    def late_weights(k):
        return pltpu.make_async_copy(ordered.at[k], late_weights_ref.at[k - early], late_weights_sem.at[k - early])

    def order(k, carry):
        load_raw(k).wait()

        @pl.when(k + 1 < per)
        def _():
            load_raw(k + 1).start(priority=1)

        wide[...] = raw[k % 2].astype(jnp.float32)
        for w in range(2):
            for tile in range(tiles_s):
                ordered[k, :, pl.ds((w * tiles_s + tile) * LANES, LANES)] = wide[
                    pl.ds(tile * 2 + w, beams, stride=rows_b), :
                ].astype(jnp.bfloat16)

        @pl.when(k >= early)
        def _():
            late_weights(k).start(priority=1)

        return carry

    lines = held.reshape(per * quads * everyone, LANES)

    def put(k):
        return pltpu.make_async_copy(
            done.at[k % 2], part_ref.at[pl.ds(pl.multiple_of(k * rows_o, rows_o), rows_o)], part_sem.at[k % 2]
        )

    def form(k, carry):
        quad = [
            lines[pl.ds(pl.multiple_of((k * quads + q) * everyone, everyone), everyone), :] for q in range(quads)
        ]
        form_beams(quad, ordered[k], values, beams, pols, spectra)

        @pl.when(k >= 2)
        def _():
            put(k).wait()

        done[k % 2] = values[...].astype(jnp.bfloat16)
        put(k).start(priority=1)
        return carry

    def before(amounts, u):
        return sum((n * (u > at).astype(jnp.int32) for at, n in enumerate(amounts) if n), jnp.int32(0))

    def turn(u, carry):
        for at, acts in enumerate(TURNS):
            if acts:

                @pl.when(u == at)
                def _():
                    for what, i in acts:
                        act(what, i)

        lax.fori_loop(before(ORDERED, u), before(ORDERED, u + 1), order, 0)
        lax.fori_loop(before(FORMED, u), before(FORMED, u + 1), form, 0)
        return carry

    lax.fori_loop(0, len(TURNS), turn, 0)
    for i in range(len(ITEMS)):
        sent(i).wait()
        for d in range(2):
            side(i, d).wait_send()
            far(i, d).wait_send()
        for e in range(5):
            mate_copy(i, e).wait_send()
    for k in range(early - 2, early):
        put(k).wait()
    for k in range(early, per):
        late_weights(k).wait()
    for i in range(len(ITEMS)):
        if ITEMS[i][0] >= early:
            late_spectra(i).wait()


def form_beams(quad, weights, values, beams, pols, spectra):
    real = jnp.concatenate([quad[p * 2] for p in range(pols)], axis=1)
    imag = jnp.concatenate([quad[p * 2 + 1] for p in range(pols)], axis=1)
    for part in range(2):
        other = jnp.concatenate([imag, real] if part else [real, -imag], axis=0)
        product = jnp.dot(weights, other, preferred_element_type=jnp.float32)
        for p in range(pols):
            values[pl.ds(p * 2 + part, beams, stride=2 * pols), :] = product[:, p * spectra : (p + 1) * spectra]


def beams_kernel(
    dims, part_hbm, spectra_hbm, weights_hbm, out_ref, part, held, ordered, values, done,
    part_in, part_out, held_sem, ordered_sem, done_sem,
):
    beams, pols, spectra, early, late = dims
    quads = 2 * pols
    rows_o = beams * quads

    def take(k):
        where = pl.ds(k * rows_o, rows_o)
        return pltpu.make_async_copy(part_hbm.at[where], part.at[where], part_in.at[k])

    def give(k):
        where = pl.ds(k * rows_o, rows_o)
        return pltpu.make_async_copy(part.at[where], out_ref.at[where], part_out.at[k])

    def spectra_of(k):
        return pltpu.make_async_copy(spectra_hbm.at[k], held.at[k], held_sem.at[k])

    def weights_of(k):
        return pltpu.make_async_copy(weights_hbm.at[k], ordered.at[k], ordered_sem.at[k])

    def put(k):
        return pltpu.make_async_copy(
            done.at[k], out_ref.at[pl.ds((early + k) * rows_o, rows_o)], done_sem.at[k]
        )

    each = -(-early // late)
    for k in range(late):
        spectra_of(k).start()
        weights_of(k).start()
    for k in range(early):
        take(k).start()
    for k in range(late):
        spectra_of(k).wait()
        weights_of(k).wait()
        form_beams([held[k, q] for q in range(quads)], ordered[k], values, beams, pols, spectra)
        done[k] = values[...].astype(jnp.bfloat16)
        put(k).start()
        for j in range(k * each, min(early, (k + 1) * each)):
            take(j).wait()
            give(j).start()
    for k in range(early):
        give(k).wait()
    for k in range(late):
        put(k).wait()


def shards(sizes, voltages, filter_taps, chan_index, beam_weights):
    n_chan, n_grp = sizes
    stations, pols, blocks, width = voltages.shape
    taps, size = filter_taps.shape
    channels = chan_index.shape[0]
    per, beams = beam_weights.shape[:2]
    everyone = beam_weights.shape[3]
    spectra = blocks - taps + 1
    tiles = size // LANES
    tiles_s = everyone // LANES
    rows_m = 2 * tiles * pols
    quads = 2 * pols
    late = LATE
    items = len(ITEMS)
    early = per - late
    beam_rows = beams * tiles_s * 2
    rows_o = beams * quads

    lines = voltages.transpose(0, 2, 1, 3).reshape(stations, blocks, pols, 2 * tiles, LANES)
    lines = lines.transpose(0, 1, 3, 2, 4).reshape(stations * blocks * rows_m, LANES)
    rows_w = beam_weights.reshape(per, beams, 2, tiles_s, LANES).transpose(0, 1, 3, 2, 4)
    rows_w = rows_w.reshape(per * beam_rows, LANES)
    index = chan_index.reshape(1, channels)
    dims = (n_chan, n_grp // 2, stations, pols, blocks, taps, size, channels, beams, late)
    spread_rows = channels * quads * stations
    dma = pltpu.SemaphoreType.DMA
    anywhere = pl.BlockSpec(memory_space=pl.ANY)
    part, held, ordered = pl.pallas_call(
        functools.partial(spectra_kernel, dims),
        out_shape=[
            jax.ShapeDtypeStruct((early * rows_o, LANES), jnp.bfloat16),
            jax.ShapeDtypeStruct((late, quads, n_chan, n_grp, stations, LANES), jnp.bfloat16),
            jax.ShapeDtypeStruct((late, beams, 2 * everyone), jnp.bfloat16),
        ],
        in_specs=[anywhere, anywhere, pl.BlockSpec(memory_space=pltpu.VMEM), anywhere, anywhere],
        out_specs=[anywhere] * 3,
        scratch_shapes=[
            pltpu.VMEM((stations * blocks * rows_m, LANES), jnp.bfloat16),
            pltpu.VMEM((taps, size), jnp.float32),
            pltpu.VMEM((size, 2 * size), jnp.bfloat16),
            pltpu.VMEM((taps * tiles * pols, LANES), jnp.float32),
            pltpu.VMEM((2 * channels, 2 * size), jnp.bfloat16),
            pltpu.VMEM((spectra * rows_m, LANES), jnp.float32),
            pltpu.VMEM((pols * spectra, 2 * size), jnp.bfloat16),
            pltpu.VMEM((spread_rows, LANES), jnp.float32),
            pltpu.VMEM((spread_rows // stations, stations, LANES), jnp.bfloat16),
            pltpu.VMEM((per, quads, n_chan, n_grp, stations, LANES), jnp.bfloat16),
            pltpu.VMEM((2, beam_rows, LANES), jnp.bfloat16),
            pltpu.VMEM((beam_rows, LANES), jnp.float32),
            pltpu.VMEM((per, beams, 2 * everyone), jnp.bfloat16),
            pltpu.VMEM((rows_o, LANES), jnp.float32),
            pltpu.VMEM((2, rows_o, LANES), jnp.bfloat16),
            dma((stations + 2,)), dma((items,)), dma((items,)), dma((items,)),
            dma((items, 2)), dma((items, 2)), dma((items, 2)), dma((items, 2)),
            dma((items, 5)), dma((items, 5)),
            dma((2,)), dma((2,)), dma((items,)), dma((late,)),
        ],
        compiler_params=pltpu.CompilerParams(
            collective_id=0, has_side_effects=True, vmem_limit_bytes=63 * 1024 * 1024
        ),
        name="spectra",
    )(lines, filter_taps, index, jnp.asarray(fourier_rows(size)), rows_w)

    out = pl.pallas_call(
        functools.partial(beams_kernel, (beams, pols, spectra, early, late)),
        out_shape=jax.ShapeDtypeStruct((per * rows_o, LANES), jnp.bfloat16),
        in_specs=[anywhere] * 3,
        out_specs=anywhere,
        scratch_shapes=[
            pltpu.VMEM((early * rows_o, LANES), jnp.bfloat16),
            pltpu.VMEM((late, quads, everyone, LANES), jnp.bfloat16),
            pltpu.VMEM((late, beams, 2 * everyone), jnp.bfloat16),
            pltpu.VMEM((rows_o, LANES), jnp.float32),
            pltpu.VMEM((late, rows_o, LANES), jnp.bfloat16),
            dma((early,)), dma((early,)), dma((late,)), dma((late,)), dma((late,)),
        ],
        compiler_params=pltpu.CompilerParams(vmem_limit_bytes=63 * 1024 * 1024),
        name="beams",
    )(part, held.reshape(late, quads, everyone, LANES), ordered)
    return out.reshape(per, beams, pols, 2, spectra)


def solution(mesh):
    sizes = (mesh.shape["chan"], mesh.shape["grp"])
    placed = (P(("chan", "grp"), None, None, None), P(), P(), P("chan", "grp", None, None))
    return jax.shard_map(
        functools.partial(shards, sizes),
        mesh=mesh,
        in_specs=placed,
        out_specs=P("chan", "grp", None, None, None),
        check_vma=False,
    )
```

```python
import functools
import math

import jax
import jax.numpy as jnp
import numpy as np
from jax import lax
from jax.experimental import pallas as pl
from jax.experimental.pallas import tpu as pltpu
from jax.sharding import PartitionSpec as P

MESH = pl.DeviceIdType.MESH
LANES = 128
ITEMS = ((0, 2), (2, 4), (4, 6), (6, 8), (8, 10), (10, 12))
AHEAD = (0, 1)
TURNS = (
    (("out", 0), ("first", 2), ("out", 1), ("first", 3)),
    (("far", 0), ("out", 2), ("first", 4)),
    (("far", 1), ("out", 3), ("first", 5), ("mate", 0)),
    (("far", 2), ("out", 4), ("mate", 1), ("all", 0)),
    (("far", 3), ("out", 5), ("mate", 2), ("all", 1)),
    (("far", 4), ("mate", 3), ("all", 2)),
    (("far", 5), ("mate", 4), ("all", 3)),
    (("mate", 5), ("late", 4), ("late", 5)),
)
FORMED = (0, 0, 0, 2, 2, 2, 2, 0)
ORDERED = (2, 4, 4, 2, 0, 0, 0, 0)
LATE = 4


def fourier_rows(size):
    steps = np.arange(size, dtype=np.int64)
    phase = (steps[:, None] * steps[None, :]) % size
    angle = np.float32(2.0 * math.pi / size) * phase.astype(np.float32)
    factor = np.float32(1.0 / math.sqrt(size))
    rows = np.concatenate([np.cos(angle) * factor, np.sin(angle) * factor], axis=1)
    return rows.astype(jnp.bfloat16)


def spectra_kernel(
    dims, volts_hbm, taps_hbm, index_ref, rows_hbm, weights_hbm, part_ref, late_ref, late_weights_ref,
    volts, taps_ref, rows_ref, tapb, table, sums, flat, spread, ready, held, raw, wide, ordered, values, done,
    load_sem, own_sem, one_send, one_recv, side_send, side_recv, far_send, far_recv, mate_send, mate_recv,
    raw_sem, part_sem, late_sem, late_weights_sem,
):
    n_chan, n_x, stations, pols, blocks, taps, size, channels, beams, late = dims
    n_grp = 2 * n_x
    spectra = blocks - taps + 1
    tiles = size // LANES
    per = channels // n_chan
    early = per - late
    quads = 2 * pols
    rows_m = 2 * tiles * pols
    everyone = n_chan * n_grp * stations
    tiles_s = everyone // LANES
    rows_b = 2 * tiles_s
    rows_w = beams * rows_b
    rows_o = beams * quads

    chan = lax.axis_index("chan")
    grp = lax.axis_index("grp")
    place = grp // 2
    core = grp % 2
    right = lax.rem(place + 1, n_x) * 2 + core
    left = lax.rem(place + n_x - 1, n_x) * 2 + core
    across = lax.rem(place + 2, n_x) * 2 + core
    mate = place * 2 + 1 - core

    def load(s):
        span = pl.ds(s * blocks * rows_m, blocks * rows_m)
        return pltpu.make_async_copy(volts_hbm.at[span], volts.at[span], load_sem.at[s])

    def load_taps():
        return pltpu.make_async_copy(taps_hbm, taps_ref, load_sem.at[stations])

    def load_rows():
        return pltpu.make_async_copy(rows_hbm, rows_ref, load_sem.at[stations + 1])

    load_taps().start()
    load(0).start()
    load_rows().start()
    for s in range(1, stations):
        load(s).start()

    def load_raw(k):
        return pltpu.make_async_copy(
            weights_hbm.at[pl.ds(pl.multiple_of(k * rows_w, rows_w), rows_w)], raw.at[k % 2], raw_sem.at[k % 2]
        )

    load_raw(0).start(priority=1)

    barrier = pltpu.get_barrier_semaphore()

    def greet(j, carry):
        other = lax.rem(chan + j, n_chan)
        pl.semaphore_signal(barrier, inc=1, device_id={"chan": other, "grp": grp}, device_id_type=MESH)
        return carry

    lax.fori_loop(1, n_chan, greet, 0)
    for other in (right, left, mate):
        pl.semaphore_signal(barrier, inc=1, device_id={"chan": chan, "grp": other}, device_id_type=MESH)

    load_taps().wait()
    for t in range(taps):
        for tile in range(tiles):
            line = taps_ref[pl.ds(t, 1), pl.ds(tile * LANES, LANES)]
            tapb[pl.ds((t * tiles + tile) * pols, pols), :] = jnp.broadcast_to(line, (pols, LANES))

    load_rows().wait()
    place_of = lax.broadcasted_iota(jnp.int32, (size, channels), 0)
    chosen = (place_of == index_ref[...]).astype(jnp.float32).astype(jnp.bfloat16)
    picked = lax.dot_general(
        chosen, rows_ref[...], (((0,), (0,)), ((), ())), preferred_element_type=jnp.float32
    )
    table[pl.ds(0, channels), :] = picked.astype(jnp.bfloat16)
    table[pl.ds(channels, channels), pl.ds(0, size)] = (-picked[:, size:]).astype(jnp.bfloat16)
    table[pl.ds(channels, channels), pl.ds(size, size)] = picked[:, :size].astype(jnp.bfloat16)

    outgoing = ready.reshape(n_chan, per, quads, stations, LANES)
    flat_spread = spread.reshape(quads * channels * stations, LANES)

    def span(i):
        return pl.ds(ITEMS[i][0], ITEMS[i][1] - ITEMS[i][0])

    def first_copy(i, other):
        return pltpu.make_async_remote_copy(
            src_ref=outgoing.at[other, span(i)],
            dst_ref=held.at[span(i), :, chan, grp],
            send_sem=one_send.at[i],
            recv_sem=one_recv.at[i],
            device_id={"chan": other, "grp": grp},
            device_id_type=MESH,
        )

    def own_copy(i):
        return pltpu.make_async_copy(outgoing.at[chan, span(i)], held.at[span(i), :, chan, grp], own_sem.at[i])

    def first_sends(i):
        def send(j, carry):
            first_copy(i, lax.rem(chan + j, n_chan)).start()
            return carry

        lax.fori_loop(1, n_chan, send, 0)
        own_copy(i).start()

    def gathered(i):
        piece = held.at[span(i), :, pl.ds(0, n_chan - 1), grp]
        return pltpu.make_async_copy(piece, piece, one_recv.at[i])

    def sent(i):
        piece = held.at[span(i), :, pl.ds(0, n_chan - 1), grp]
        return pltpu.make_async_copy(piece, piece, one_send.at[i])

    def grp_copy(i, part, owner, to, send_sem, recv_sem):
        quad = slice(None) if part is None else pl.ds(part * pols, pols)
        piece = held.at[span(i), quad, :, owner]
        return pltpu.make_async_remote_copy(
            src_ref=piece, dst_ref=piece, send_sem=send_sem, recv_sem=recv_sem,
            device_id={"chan": chan, "grp": to}, device_id_type=MESH,
        )

    def side(i, d):
        return grp_copy(i, None, grp, (right, left)[d], side_send.at[i, d], side_recv.at[i, d])

    def side_in(i, d):
        return grp_copy(i, None, (left, right)[d], right, side_send.at[i, d], side_recv.at[i, d])

    def far(i, d):
        return grp_copy(i, d, (left, right)[d], (right, left)[d], far_send.at[i, d], far_recv.at[i, d])

    def far_in(i, d):
        return grp_copy(i, d, across, right, far_send.at[i, d], far_recv.at[i, d])

    def mate_copy(i, e):
        sems = (mate_send.at[i, e], mate_recv.at[i, e])
        if e == 0:
            return grp_copy(i, None, grp, mate, *sems)
        if e < 3:
            return grp_copy(i, None, (left, right)[e - 1], mate, *sems)
        return grp_copy(i, e - 3, across, mate, *sems)

    def mate_in(i, e):
        shift = 1 - 2 * core
        sems = (mate_send.at[i, e], mate_recv.at[i, e])
        if e == 0:
            return grp_copy(i, None, mate, mate, *sems)
        if e < 3:
            return grp_copy(i, None, (left, right)[e - 1] + shift, mate, *sems)
        return grp_copy(i, e - 3, across + shift, mate, *sems)

    def late_spectra(i):
        low, high = ITEMS[i]
        return pltpu.make_async_copy(
            held.at[pl.ds(low, high - low)], late_ref.at[pl.ds(low - early, high - low)], late_sem.at[i]
        )

    def out(i):
        own_copy(i).wait()
        gathered(i).wait()
        for d in range(2):
            side(i, d).start()
        mate_copy(i, 0).start()

    def act(what, i):
        if what == "out":
            out(i)
        if what == "first":
            first_sends(i)
        for d in range(2):
            if what == "far":
                side_in(i, d).wait_recv()
                far(i, d).start()
                mate_copy(i, 1 + d).start()
            if what == "mate":
                far_in(i, d).wait_recv()
                mate_copy(i, 3 + d).start()
        if what in ("all", "late"):
            for e in range(5):
                mate_in(i, e).wait_recv()
        if what == "late":
            late_spectra(i).start(priority=1)

    group = 8
    half = tiles * pols
    for s in range(stations):
        load(s).wait()

        def filter_group(i, carry):
            first = i * group
            coefs = [tapb[pl.ds(t * half, half), :] for t in range(taps)]
            views = []
            for m in range(group + taps - 1):
                start = pl.multiple_of((s * blocks + first + m) * rows_m, rows_m)
                views.append(volts[pl.ds(start, rows_m), :].astype(jnp.float32))
            both = [coefs[2 * j] + coefs[2 * j + 1] for j in range(taps // 2)]
            for part in range(2):
                side_of = [view[part * half : (part + 1) * half] for view in views]

                def chain(values, factors):
                    total = values[0] * factors[0]
                    for value, factor in zip(values[1:], factors[1:]):
                        total = total + value * factor
                    return total

                joined = [side_of[m] + side_of[m + 1] for m in range(1, group + taps - 2, 2)]
                before_it = chain(side_of[0 : taps : 2], coefs[0::2])
                for i in range(group // 2):
                    odd = chain(side_of[2 * i + 1 : 2 * i + 1 + taps : 2], coefs[1::2])
                    after_it = chain(side_of[2 * i + 2 : 2 * i + 2 + taps : 2][: taps // 2], coefs[0::2])
                    cross = chain(joined[i : i + taps // 2], both)
                    for m, total in ((0, before_it + odd), (1, (cross - odd) - after_it)):
                        for j in range(half // 4):
                            at = pl.multiple_of(first * 4, group * 4) + (
                                (part * (half // 4) + j) * spectra + 2 * i + m
                            ) * 4
                            sums[pl.ds(at, 4), :] = total[j * 4 : (j + 1) * 4]
                    before_it = after_it
            return carry

        lax.fori_loop(0, spectra // group, filter_group, 0)
        for p in range(pols):
            for part in range(2):
                for tile in range(tiles):
                    line = part * half + tile * pols + p
                    line = line // 4 * spectra * 4 + line % 4
                    flat[pl.ds(p * spectra, spectra), pl.ds((part * tiles + tile) * LANES, LANES)] = sums[
                        pl.ds(line, spectra, stride=4), :
                    ].astype(jnp.bfloat16)
        product = sum(
            lax.dot_general(
                table[:, part * size : (part + 1) * size],
                flat[:, part * size : (part + 1) * size],
                (((1,), (1,)), ((), ())),
                preferred_element_type=jnp.float32,
            )
            for part in range(2)
        )
        for p in range(pols):
            for part in range(2):
                line = (p * 2 + part) * channels * stations + s
                flat_spread[pl.ds(line, channels, stride=stations), :] = product[
                    part * channels : (part + 1) * channels, p * spectra : (p + 1) * spectra
                ]

    by_channel = ready.reshape(channels, quads, stations, LANES)

    def pack(k, carry):
        where = pl.ds(pl.multiple_of(k * 16, 16), 16)
        for q in range(quads):
            by_channel[where, q] = spread[q, where].astype(jnp.bfloat16)
        return carry

    lax.fori_loop(0, channels // 16, pack, 0)
    pl.semaphore_wait(barrier, n_chan + 2)
    for i in AHEAD:
        first_sends(i)

    def late_weights(k):
        return pltpu.make_async_copy(ordered.at[k], late_weights_ref.at[k - early], late_weights_sem.at[k - early])

    def order(k, carry):
        load_raw(k).wait()

        @pl.when(k + 1 < per)
        def _():
            load_raw(k + 1).start(priority=1)

        wide[...] = raw[k % 2].astype(jnp.float32)
        for w in range(2):
            for tile in range(tiles_s):
                ordered[k, :, pl.ds((w * tiles_s + tile) * LANES, LANES)] = wide[
                    pl.ds(tile * 2 + w, beams, stride=rows_b), :
                ].astype(jnp.bfloat16)

        @pl.when(k >= early)
        def _():
            late_weights(k).start(priority=1)

        return carry

    lines = held.reshape(per * quads * everyone, LANES)

    def put(k):
        return pltpu.make_async_copy(
            done.at[k % 2], part_ref.at[pl.ds(pl.multiple_of(k * rows_o, rows_o), rows_o)], part_sem.at[k % 2]
        )

    def form(k, carry):
        quad = [
            lines[pl.ds(pl.multiple_of((k * quads + q) * everyone, everyone), everyone), :] for q in range(quads)
        ]
        form_beams(quad, ordered[k], values, beams, pols, spectra)

        @pl.when(k >= 2)
        def _():
            put(k).wait()

        done[k % 2] = values[...].astype(jnp.bfloat16)
        put(k).start(priority=1)
        return carry

    def before(amounts, u):
        return sum((n * (u > at).astype(jnp.int32) for at, n in enumerate(amounts) if n), jnp.int32(0))

    def turn(u, carry):
        for at, acts in enumerate(TURNS):
            if acts:

                @pl.when(u == at)
                def _():
                    for what, i in acts:
                        act(what, i)

        lax.fori_loop(before(ORDERED, u), before(ORDERED, u + 1), order, 0)
        lax.fori_loop(before(FORMED, u), before(FORMED, u + 1), form, 0)
        return carry

    lax.fori_loop(0, len(TURNS), turn, 0)
    for i in range(len(ITEMS)):
        sent(i).wait()
        for d in range(2):
            side(i, d).wait_send()
            far(i, d).wait_send()
        for e in range(5):
            mate_copy(i, e).wait_send()
    for k in range(early - 2, early):
        put(k).wait()
    for k in range(early, per):
        late_weights(k).wait()
    for i in range(len(ITEMS)):
        if ITEMS[i][0] >= early:
            late_spectra(i).wait()


def form_beams(quad, weights, values, beams, pols, spectra):
    real = jnp.concatenate([quad[p * 2] for p in range(pols)], axis=1)
    imag = jnp.concatenate([quad[p * 2 + 1] for p in range(pols)], axis=1)
    for part in range(2):
        other = jnp.concatenate([imag, real] if part else [real, -imag], axis=0)
        product = jnp.dot(weights, other, preferred_element_type=jnp.float32)
        for p in range(pols):
            values[pl.ds(p * 2 + part, beams, stride=2 * pols), :] = product[:, p * spectra : (p + 1) * spectra]


def beams_kernel(
    dims, part_hbm, spectra_hbm, weights_hbm, out_ref, part, held, ordered, values, done,
    part_in, part_out, held_sem, ordered_sem, done_sem,
):
    beams, pols, spectra, early, late = dims
    quads = 2 * pols
    rows_o = beams * quads

    def take(k):
        where = pl.ds(k * rows_o, rows_o)
        return pltpu.make_async_copy(part_hbm.at[where], part.at[where], part_in.at[k])

    def give(k):
        where = pl.ds(k * rows_o, rows_o)
        return pltpu.make_async_copy(part.at[where], out_ref.at[where], part_out.at[k])

    def spectra_of(k):
        return pltpu.make_async_copy(spectra_hbm.at[k], held.at[k], held_sem.at[k])

    def weights_of(k):
        return pltpu.make_async_copy(weights_hbm.at[k], ordered.at[k], ordered_sem.at[k])

    def put(k):
        return pltpu.make_async_copy(
            done.at[k], out_ref.at[pl.ds((early + k) * rows_o, rows_o)], done_sem.at[k]
        )

    each = -(-early // late)
    for k in range(late):
        spectra_of(k).start()
        weights_of(k).start()
    for k in range(early):
        take(k).start()
    for k in range(late):
        spectra_of(k).wait()
        weights_of(k).wait()
        form_beams([held[k, q] for q in range(quads)], ordered[k], values, beams, pols, spectra)
        done[k] = values[...].astype(jnp.bfloat16)
        put(k).start()
        for j in range(k * each, min(early, (k + 1) * each)):
            take(j).wait()
            give(j).start()
    for k in range(early):
        give(k).wait()
    for k in range(late):
        put(k).wait()


def shards(sizes, voltages, filter_taps, chan_index, beam_weights):
    n_chan, n_grp = sizes
    stations, pols, blocks, width = voltages.shape
    taps, size = filter_taps.shape
    channels = chan_index.shape[0]
    per, beams = beam_weights.shape[:2]
    everyone = beam_weights.shape[3]
    spectra = blocks - taps + 1
    tiles = size // LANES
    tiles_s = everyone // LANES
    rows_m = 2 * tiles * pols
    quads = 2 * pols
    late = LATE
    items = len(ITEMS)
    early = per - late
    beam_rows = beams * tiles_s * 2
    rows_o = beams * quads

    lines = voltages.transpose(0, 2, 1, 3).reshape(stations, blocks, pols, 2 * tiles, LANES)
    lines = lines.transpose(0, 1, 3, 2, 4).reshape(stations * blocks * rows_m, LANES)
    rows_w = beam_weights.reshape(per, beams, 2, tiles_s, LANES).transpose(0, 1, 3, 2, 4)
    rows_w = rows_w.reshape(per * beam_rows, LANES)
    index = chan_index.reshape(1, channels)
    dims = (n_chan, n_grp // 2, stations, pols, blocks, taps, size, channels, beams, late)
    spread_rows = channels * quads * stations
    dma = pltpu.SemaphoreType.DMA
    anywhere = pl.BlockSpec(memory_space=pl.ANY)
    part, held, ordered = pl.pallas_call(
        functools.partial(spectra_kernel, dims),
        out_shape=[
            jax.ShapeDtypeStruct((early * rows_o, LANES), jnp.bfloat16),
            jax.ShapeDtypeStruct((late, quads, n_chan, n_grp, stations, LANES), jnp.bfloat16),
            jax.ShapeDtypeStruct((late, beams, 2 * everyone), jnp.bfloat16),
        ],
        in_specs=[anywhere, anywhere, pl.BlockSpec(memory_space=pltpu.VMEM), anywhere, anywhere],
        out_specs=[anywhere] * 3,
        scratch_shapes=[
            pltpu.VMEM((stations * blocks * rows_m, LANES), jnp.bfloat16),
            pltpu.VMEM((taps, size), jnp.float32),
            pltpu.VMEM((size, 2 * size), jnp.bfloat16),
            pltpu.VMEM((taps * tiles * pols, LANES), jnp.float32),
            pltpu.VMEM((2 * channels, 2 * size), jnp.bfloat16),
            pltpu.VMEM((spectra * rows_m, LANES), jnp.float32),
            pltpu.VMEM((pols * spectra, 2 * size), jnp.bfloat16),
            pltpu.VMEM((quads, channels, stations, LANES), jnp.float32),
            pltpu.VMEM((spread_rows // stations, stations, LANES), jnp.bfloat16),
            pltpu.VMEM((per, quads, n_chan, n_grp, stations, LANES), jnp.bfloat16),
            pltpu.VMEM((2, beam_rows, LANES), jnp.bfloat16),
            pltpu.VMEM((beam_rows, LANES), jnp.float32),
            pltpu.VMEM((per, beams, 2 * everyone), jnp.bfloat16),
            pltpu.VMEM((rows_o, LANES), jnp.float32),
            pltpu.VMEM((2, rows_o, LANES), jnp.bfloat16),
            dma((stations + 2,)), dma((items,)), dma((items,)), dma((items,)),
            dma((items, 2)), dma((items, 2)), dma((items, 2)), dma((items, 2)),
            dma((items, 5)), dma((items, 5)),
            dma((2,)), dma((2,)), dma((items,)), dma((late,)),
        ],
        compiler_params=pltpu.CompilerParams(
            collective_id=0, has_side_effects=True, vmem_limit_bytes=63 * 1024 * 1024
        ),
        name="spectra",
    )(lines, filter_taps, index, jnp.asarray(fourier_rows(size)), rows_w)

    out = pl.pallas_call(
        functools.partial(beams_kernel, (beams, pols, spectra, early, late)),
        out_shape=jax.ShapeDtypeStruct((per * rows_o, LANES), jnp.bfloat16),
        in_specs=[anywhere] * 3,
        out_specs=anywhere,
        scratch_shapes=[
            pltpu.VMEM((early * rows_o, LANES), jnp.bfloat16),
            pltpu.VMEM((late, quads, everyone, LANES), jnp.bfloat16),
            pltpu.VMEM((late, beams, 2 * everyone), jnp.bfloat16),
            pltpu.VMEM((rows_o, LANES), jnp.float32),
            pltpu.VMEM((late, rows_o, LANES), jnp.bfloat16),
            dma((early,)), dma((early,)), dma((late,)), dma((late,)), dma((late,)),
        ],
        compiler_params=pltpu.CompilerParams(vmem_limit_bytes=63 * 1024 * 1024),
        name="beams",
    )(part, held.reshape(late, quads, everyone, LANES), ordered)
    return out.reshape(per, beams, pols, 2, spectra)


def solution(mesh):
    sizes = (mesh.shape["chan"], mesh.shape["grp"])
    placed = (P(("chan", "grp"), None, None, None), P(), P(), P("chan", "grp", None, None))
    return jax.shard_map(
        functools.partial(shards, sizes),
        mesh=mesh,
        in_specs=placed,
        out_specs=P("chan", "grp", None, None, None),
        check_vma=False,
    )
```
